32 devices in a mesh: days: 2 (over y), sta: 8 (over z, x), win: 2 (over core).
Axes of the slice: x: 2, y: 2, z: 4, core: 2. Of those that a mesh axis runs over, the one named last changes fastest.
Arguments:
- phases: bfloat16 [48, 2048, 16], P(('days', 'win'), 'sta'), parts along dimension 0, may hold values from -3.140625 to 3.140625
- window_valid: int32 [48], P('days'), parts along dimension 0, may hold values 0 or 1
- freq_taper: float32 [2048], replicated, may hold values from 0.1 to 1.9
- pair_mask: int32 [8, 8], replicated, may hold values from 0 to 1, as said below
Outputs:
- correlations: float32 [32, 16, 512], P(('days', 'sta'), None, 'win'), parts along dimension 0
The draws below stay inside these ranges and needn't reach their ends.
There are 2 independent parts, one for each index of `days`. The reference program is written for one: setup_inputs(seed, part) draws one part's arguments, and reference() takes and returns one part's arrays. A program takes and returns all parts, laid end to end along the dimension named above; an argument that names none is the same for every part. Nothing has to cross between parts.
Inputs may be any that keep to these rules, and one draw needn't show every extreme that they name: `pair_mask`: symmetric over the two block indices; every diagonal block is kept.
All inputs are finite; a program needn't handle non-finite values.
Results may differ from the reference program's by a relative error of at most 0.005.
Values may be sent and summed in bfloat16 or wider, within the bound.
A program may use at most 64 MiB of HBM per device.

```python
import math
import jax
import jax.numpy as jnp
from jax import lax

F = 2048
LAGS = 512
WL = 12
SDEV = 2
WINDOWS = 24
STATIONS = 16
NBLK = 8
N_STA = 8
N_WIN = 2


def draw_pair_mask(key, part):
    raw_bits = jax.random.randint(key, (NBLK, NBLK), 0, 2).astype(jnp.int32)
    row_index = jnp.arange(NBLK, dtype=jnp.int32)[:, None]
    col_index = jnp.arange(NBLK, dtype=jnp.int32)[None, :]
    symmetric = jnp.where(row_index <= col_index, raw_bits, raw_bits.T)
    return jnp.where(row_index == col_index, 1, symmetric).astype(jnp.int32)


def place_ends(result, own_key, least, largest):
    spot = [jax.random.randint(jax.random.fold_in(own_key, axis), (), 0, length) for axis, length in enumerate(result.shape)]
    widest = result.shape.index(max(result.shape))
    beside = spot[:widest] + [(spot[widest] + 1) % result.shape[widest]] + spot[widest + 1:]
    return result.at[tuple(spot)].set(least).at[tuple(beside)].set(largest)


def setup_inputs(seed: int = 0, part: int = 0) -> dict:
    splits = jax.random.split(jax.random.key(seed), 5)
    part_keys = jax.random.split(jax.random.fold_in(splits[4], part), 5)
    phases = jnp.clip(jax.random.uniform(part_keys[0], (WINDOWS, F, STATIONS), jnp.float32, -3.140625, 3.140625), -3.140625, 3.140625).astype(jnp.bfloat16)
    window_valid = place_ends((jax.random.randint(part_keys[1], (WINDOWS,), 0, 4) < 3).astype(jnp.int32), jax.random.fold_in(part_keys[1], 1), 0, 1)
    freq_taper = jnp.clip(1.0 + 0.18 * jax.random.normal(splits[2], (F,), jnp.float32), 0.1, 1.9)
    pair_mask = draw_pair_mask(jax.random.fold_in(splits[4], 71), part)
    return {"phases": phases, "window_valid": window_valid, "freq_taper": freq_taper, "pair_mask": pair_mask}


def lag_table(freq_bins, lag_count):
    freq_index = jnp.arange(freq_bins, dtype=jnp.int32)[:, None]
    lag_index = jnp.arange(lag_count, dtype=jnp.int32)[None, :] - lag_count // 2
    wrapped = jnp.mod(freq_index * lag_index, 2 * freq_bins)
    angle = wrapped.astype(jnp.float32) * (math.pi / freq_bins)
    return jnp.stack((jnp.cos(angle), -jnp.sin(angle))).astype(jnp.bfloat16)

def rounded(values):
    return lax.optimization_barrier(values.astype(jnp.bfloat16)).astype(jnp.float32)

def reference(phases, window_valid, freq_taper, pair_mask):
    phase_f = phases.astype(jnp.float32)
    phasor_cos = rounded(jnp.cos(phase_f)).reshape(N_WIN, WL, F, STATIONS)
    phasor_sin = rounded(jnp.sin(phase_f)).reshape(N_WIN, WL, F, STATIONS)
    valid_f = window_valid.astype(jnp.float32)
    valid_count = jnp.sum(valid_f)
    norm_scale = 1.0 / jnp.sqrt(F * jnp.maximum(valid_count, 1.0))
    valid_groups = valid_f.reshape(N_WIN, WL)[:, :, None, None]
    weighted_cos = phasor_cos * valid_groups
    weighted_sin = phasor_sin * valid_groups
    bin_weight = freq_taper.astype(jnp.float32) * norm_scale
    lag_f = lag_table(F, LAGS).astype(jnp.float32)
    keep_full = jnp.repeat(jnp.repeat(pair_mask, SDEV, 0), SDEV, 1).astype(jnp.float32)
    keep_full = keep_full * (1.0 - jnp.eye(STATIONS, dtype=jnp.float32))
    highest = lax.Precision.HIGHEST

    def one_block(index):
        start = index * SDEV
        recv_cos = lax.dynamic_slice_in_dim(weighted_cos, start, SDEV, 3)
        recv_sin = lax.dynamic_slice_in_dim(weighted_sin, start, SDEV, 3)
        cross_re = jnp.einsum('gwki,gwkj->gijk', recv_cos, phasor_cos, precision=highest)
        cross_re = cross_re + jnp.einsum('gwki,gwkj->gijk', recv_sin, phasor_sin, precision=highest)
        cross_im = jnp.einsum('gwki,gwkj->gijk', recv_sin, phasor_cos, precision=highest)
        cross_im = cross_im - jnp.einsum('gwki,gwkj->gijk', recv_cos, phasor_sin, precision=highest)
        spec_re = lax.optimization_barrier(jnp.sum(rounded(cross_re * bin_weight), axis=0))
        spec_im = lax.optimization_barrier(jnp.sum(rounded(cross_im * bin_weight), axis=0))
        stacked = jnp.stack((spec_re, spec_im))
        correlation = jnp.einsum('cijk,ckt->ijt', stacked, lag_f, precision=highest)
        pair_keep = lax.dynamic_slice_in_dim(keep_full, start, SDEV, 0)
        return correlation * pair_keep[:, :, None]
    blocks = lax.map(one_block, jnp.arange(N_STA, dtype=jnp.int32))
    return blocks.reshape(STATIONS, STATIONS, LAGS)
```

```python
import math

import jax
import jax.numpy as jnp
import numpy as np
from jax import lax
from jax.experimental import pallas as pl
from jax.experimental.pallas import tpu as pltpu
from jax.sharding import PartitionSpec as P

LAGS = 512
MESH = pl.DeviceIdType.MESH


def fit(function, degree):
    nodes = np.polynomial.chebyshev.Chebyshev.interpolate(function, degree, domain=[0.0, math.pi**2])
    return [float(c) for c in nodes.convert(kind=np.polynomial.Polynomial).coef]


def sinc_of_square(y):
    x = np.sqrt(y)
    return np.sinc(x / math.pi)


SIN_COEF = fit(sinc_of_square, 7)
COS_COEF = fit(lambda y: np.cos(np.sqrt(y)), 8)


def horner(coef, y):
    total = jnp.full_like(y, coef[-1])
    for c in coef[-2::-1]:
        total = total * y + c
    return total


def cos_sin(x):
    y = x * x
    return horner(COS_COEF, y), x * horner(SIN_COEF, y)


def fused_kernel(
    phases_ref,
    valid_ref,
    taper_ref,
    mask_ref,
    out_ref,
    cos_ref,
    sin_ref,
    spec_re,
    spec_im,
    lag_cos,
    lag_sin,
    own,
    swap_out,
    swap_in,
    send,
    recv,
    swap_send_sem,
    swap_recv_sem,
    send_sem,
    recv_sem,
    *,
    sta_count,
):
    days, sta, win = (lax.axis_index(a) for a in ("days", "sta", "win"))
    win_rows, stations, band = phases_ref.shape
    recv_rows = stations // sta_count
    block = recv_rows * stations
    freq_bins = band * sta_count
    half = LAGS // 2

    barrier = pltpu.get_barrier_semaphore()
    pl.semaphore_signal(barrier, inc=1, device_id=(days, sta, 1 - win), device_id_type=MESH)
    for step in range(1, sta_count):
        peer = lax.rem(sta + step, sta_count)
        pl.semaphore_signal(barrier, inc=1, device_id=(days, peer, win), device_id_type=MESH)

    @pl.loop(0, win_rows)
    def _(w):
        weight = valid_ref[win * win_rows + w].astype(jnp.float32)
        c, s = cos_sin(phases_ref[w].astype(jnp.float32))
        cos_ref[w] = c.astype(jnp.bfloat16).astype(jnp.float32) * weight
        sin_ref[w] = s.astype(jnp.bfloat16).astype(jnp.float32) * weight

    rows = 16
    lag = lax.broadcasted_iota(jnp.int32, (rows, LAGS), 1) - half
    sub = lax.broadcasted_iota(jnp.int32, (rows, LAGS), 0)

    @pl.loop(0, band // rows)
    def _(b):
        k = sub + (sta * band + b * rows)
        turn = ((k * lag + freq_bins) & (2 * freq_bins - 1)) - freq_bins
        c, s = cos_sin(turn.astype(jnp.float32) * (math.pi / freq_bins))
        at = pl.ds(pl.multiple_of(b * rows, rows), rows)
        lag_cos[at, :] = c.astype(jnp.bfloat16)
        lag_sin[at, :] = (-s).astype(jnp.bfloat16)

    count = valid_ref[0]
    for w in range(1, valid_ref.shape[0]):
        count = count + valid_ref[w]
    count = jnp.full((1, 128), count, jnp.int32).astype(jnp.float32)
    norm = 1.0 / jnp.sqrt(freq_bins * jnp.maximum(count, 1.0))
    lane_rows = band // 128
    weight = jnp.concatenate(
        [taper_ref[pl.ds(sta * lane_rows + r, 1), :] * norm for r in range(lane_rows)], axis=1
    )

    @pl.loop(0, stations // 2)
    def _(p):
        re = [jnp.zeros((stations, band), jnp.float32) for _ in range(2)]
        im = [jnp.zeros((stations, band), jnp.float32) for _ in range(2)]
        for w in range(win_rows):
            cj, sj = cos_ref[w], sin_ref[w]
            for q in range(2):
                ci = cos_ref[w, pl.ds(2 * p + q, 1), :]
                si = sin_ref[w, pl.ds(2 * p + q, 1), :]
                re[q] = re[q] + (ci * cj + si * sj)
                im[q] = im[q] + (si * cj - ci * sj)
        for q in range(2):
            at = pl.ds(pl.multiple_of((2 * p + q) * stations, stations), stations)
            spec_re[at, :] = (re[q] * weight).astype(jnp.bfloat16)
            spec_im[at, :] = (im[q] * weight).astype(jnp.bfloat16)

    def to_lags(which):
        at = pl.ds(pl.multiple_of(which * half, half), half)
        part = jnp.dot(spec_re[...], lag_cos[:, at], preferred_element_type=jnp.float32)
        return part + jnp.dot(spec_im[...], lag_sin[:, at], preferred_element_type=jnp.float32)

    other = to_lags(1 - win).astype(jnp.bfloat16)
    for b in range(sta_count):
        swap_out[b] = other[b * block : (b + 1) * block]
    pl.semaphore_wait(barrier, sta_count)

    def swap(step):
        peer = lax.rem(sta + step, sta_count)
        return pltpu.make_async_remote_copy(
            src_ref=swap_out.at[peer],
            dst_ref=swap_in.at[peer],
            send_sem=swap_send_sem.at[step],
            recv_sem=swap_recv_sem.at[step],
            device_id=(days, sta, 1 - win),
            device_id_type=MESH,
        )

    def scatter(step):
        peer = lax.rem(sta + step, sta_count)
        return pltpu.make_async_remote_copy(
            src_ref=send.at[peer],
            dst_ref=recv.at[step],
            send_sem=send_sem.at[step],
            recv_sem=recv_sem.at[step],
            device_id=(days, peer, win),
            device_id_type=MESH,
        )

    order = sorted(range(1, sta_count), key=lambda n: abs(n - sta_count // 2)) + [0]
    for step in order:
        swap(step).start()
    mine = to_lags(win)
    for b in range(sta_count):
        own[b] = mine[b * block : (b + 1) * block]
    for step in order:
        peer = lax.rem(sta + step, sta_count)
        swap(step).wait_recv()
        total = own[peer] + swap_in[peer].astype(jnp.float32)
        if step:
            send[peer] = total.astype(jnp.bfloat16)
            scatter(step).start()
    for step in order[::-1][1:]:
        scatter(step).wait_recv()
        total = total + recv[step].astype(jnp.float32)

    source = lax.broadcasted_iota(jnp.int32, (stations, half), 0)
    keep = jnp.zeros((stations, half), jnp.float32)
    for b in range(sta_count):
        keep = jnp.where(source // recv_rows == b, mask_ref[sta, b].astype(jnp.float32), keep)
    for r in range(recv_rows):
        pair_keep = jnp.where(source == sta * recv_rows + r, 0.0, keep)
        out_ref[r] = total[r * stations : (r + 1) * stations] * pair_keep
    for step in order:
        swap(step).wait_send()
        if step:
            scatter(step).wait_send()


def fused(phases, window_valid, freq_taper, pair_mask):
    sta_count = lax.axis_size("sta")
    win_rows, band, stations = phases.shape
    recv_rows = stations // sta_count
    block = recv_rows * stations
    pairs = stations * stations
    half = LAGS // 2
    f32, bf16, vmem = jnp.float32, jnp.bfloat16, pltpu.VMEM
    in_vmem, in_smem = pl.BlockSpec(memory_space=pltpu.VMEM), pl.BlockSpec(memory_space=pltpu.SMEM)
    return pl.pallas_call(
        lambda *refs: fused_kernel(*refs, sta_count=sta_count),
        name="fused",
        out_shape=jax.ShapeDtypeStruct((recv_rows, stations, half), f32),
        in_specs=[in_vmem, in_smem, in_vmem, in_smem],
        out_specs=in_vmem,
        scratch_shapes=[
            vmem((win_rows, stations, band), f32),
            vmem((win_rows, stations, band), f32),
            vmem((pairs, band), bf16),
            vmem((pairs, band), bf16),
            vmem((band, LAGS), bf16),
            vmem((band, LAGS), bf16),
            vmem((sta_count, block, half), f32),
            vmem((sta_count, block, half), bf16),
            vmem((sta_count, block, half), bf16),
            vmem((sta_count, block, half), bf16),
            vmem((sta_count, block, half), bf16),
            pltpu.SemaphoreType.DMA((sta_count,)),
            pltpu.SemaphoreType.DMA((sta_count,)),
            pltpu.SemaphoreType.DMA((sta_count,)),
            pltpu.SemaphoreType.DMA((sta_count,)),
        ],
        compiler_params=pltpu.CompilerParams(collective_id=0, has_side_effects=True),
    )(
        jnp.transpose(phases, (0, 2, 1)),
        window_valid,
        freq_taper.reshape(-1, 128),
        pair_mask,
    )


def lag_table(freq_bins, lag_count):
    freq_index = jnp.arange(freq_bins, dtype=jnp.int32)[:, None]
    lag_index = jnp.arange(lag_count, dtype=jnp.int32)[None, :] - lag_count // 2
    wrapped = jnp.mod(freq_index * lag_index, 2 * freq_bins)
    angle = wrapped.astype(jnp.float32) * (math.pi / freq_bins)
    return jnp.stack((jnp.cos(angle), -jnp.sin(angle))).astype(jnp.bfloat16)


def per_device(phases, window_valid, freq_taper, pair_mask):
    sta_count = lax.axis_size("sta")
    win_rows, band_bins, stations = phases.shape
    freq_bins = band_bins * sta_count
    recv_rows = stations // sta_count
    sta_index = lax.axis_index("sta")
    win_group = lax.axis_index("win")
    valid_count = jnp.sum(window_valid.astype(jnp.float32))
    norm_scale = 1.0 / jnp.sqrt(freq_bins * jnp.maximum(valid_count, 1.0))
    bin_weight = freq_taper * norm_scale
    group_valid = lax.dynamic_slice_in_dim(window_valid, win_group * win_rows, win_rows)
    group_weight = group_valid.astype(jnp.bfloat16)[:, None, None]
    own_f = phases.astype(jnp.float32)
    own_cos = jnp.cos(own_f).astype(jnp.bfloat16)
    own_sin = jnp.sin(own_f).astype(jnp.bfloat16)
    left_cos = own_cos * group_weight
    left_sin = own_sin * group_weight
    band_weight = lax.dynamic_slice_in_dim(bin_weight, sta_index * band_bins, band_bins)
    pair_re = jnp.einsum("wki,wkj->ijk", left_cos, own_cos, preferred_element_type=jnp.float32)
    pair_re = pair_re + jnp.einsum(
        "wki,wkj->ijk", left_sin, own_sin, preferred_element_type=jnp.float32
    )
    band_re = (pair_re * band_weight).astype(jnp.bfloat16)
    pair_im = jnp.einsum("wki,wkj->ijk", left_sin, own_cos, preferred_element_type=jnp.float32)
    pair_im = pair_im - jnp.einsum(
        "wki,wkj->ijk", left_cos, own_sin, preferred_element_type=jnp.float32
    )
    band_im = (pair_im * band_weight).astype(jnp.bfloat16)
    spectra = lax.all_to_all(
        jnp.stack((band_re, band_im)), "sta", split_axis=1, concat_axis=3, tiled=True
    )
    lag_count = LAGS
    transform = lag_table(freq_bins, lag_count)
    flat_spectra = spectra.reshape(2, recv_rows * stations, freq_bins)
    correlation = jnp.einsum(
        "cnk,ckt->nt", flat_spectra, transform, preferred_element_type=jnp.float32
    )
    block_row = lax.dynamic_index_in_dim(pair_mask, sta_index, 0, keepdims=False)
    station_row = jnp.repeat(block_row, recv_rows).astype(jnp.float32)
    receiver = sta_index * recv_rows + jnp.arange(recv_rows, dtype=jnp.int32)
    distinct = (receiver[:, None] != jnp.arange(stations, dtype=jnp.int32)[None, :]).astype(
        jnp.float32
    )
    pair_keep = station_row[None, :] * distinct
    correlation = correlation.reshape(recv_rows, stations, lag_count) * pair_keep[:, :, None]
    return lax.psum_scatter(correlation, "win", scatter_dimension=2, tiled=True)


def solution(mesh):
    def body(phases, window_valid, freq_taper, pair_mask):
        win_rows, band, stations = phases.shape
        sta_count, win_count = mesh.shape["sta"], mesh.shape["win"]
        power = band * sta_count & (band * sta_count - 1) == 0
        if band % 128 == 0 and stations % 16 == 0 and win_count == 2 and power:
            return fused(phases, window_valid, freq_taper, pair_mask)
        return per_device(phases, window_valid, freq_taper, pair_mask)

    return jax.shard_map(
        body,
        mesh=mesh,
        in_specs=(P(("days", "win"), "sta", None), P("days"), P(), P()),
        out_specs=P(("days", "sta"), None, "win"),
        check_vma=False,
    )
```

```python
import math

import jax
import jax.numpy as jnp
import numpy as np
from jax import lax
from jax.experimental import pallas as pl
from jax.experimental.pallas import tpu as pltpu
from jax.sharding import PartitionSpec as P

LAGS = 512
MESH = pl.DeviceIdType.MESH


def fit(function, degree):
    nodes = np.polynomial.chebyshev.Chebyshev.interpolate(function, degree, domain=[0.0, math.pi**2])
    return [float(c) for c in nodes.convert(kind=np.polynomial.Polynomial).coef]


def sinc_of_square(y):
    x = np.sqrt(y)
    return np.sinc(x / math.pi)


SIN_COEF = fit(sinc_of_square, 7)
COS_COEF = fit(lambda y: np.cos(np.sqrt(y)), 8)


def horner(coef, y):
    total = jnp.full_like(y, coef[-1])
    for c in coef[-2::-1]:
        total = total * y + c
    return total


def cos_sin(x):
    y = x * x
    return horner(COS_COEF, y), x * horner(SIN_COEF, y)


def fused_kernel(
    phases_hbm,
    valid_hbm,
    taper_hbm,
    mask_hbm,
    out_ref,
    phases_ref,
    valid_ref,
    taper_ref,
    mask_ref,
    load_sem,
    cos_ref,
    sin_ref,
    spec_re,
    spec_im,
    lag_cos,
    lag_sin,
    own,
    swap_out,
    swap_in,
    send,
    recv,
    swap_send_sem,
    swap_recv_sem,
    send_sem,
    recv_sem,
    *,
    sta_count,
):
    days, sta, win = (lax.axis_index(a) for a in ("days", "sta", "win"))
    win_rows, stations, band = phases_hbm.shape
    recv_rows = stations // sta_count
    block = recv_rows * stations
    freq_bins = band * sta_count
    half = LAGS // 2

    loads = [
        pltpu.make_async_copy(source, target, load_sem.at[n])
        for n, (source, target) in enumerate(
            (
                (phases_hbm, phases_ref),
                (valid_hbm, valid_ref),
                (taper_hbm, taper_ref),
                (mask_hbm, mask_ref),
            )
        )
    ]
    for load in loads:
        load.start()
    def across(step):
        peer = sta
        for bit in range(step.bit_length()):
            if step >> bit & 1:
                peer = peer + 2**bit * (1 - 2 * lax.rem(sta // 2**bit, 2))
        return peer

    barrier = pltpu.get_barrier_semaphore()
    pl.semaphore_signal(barrier, inc=1, device_id=(days, sta, 1 - win), device_id_type=MESH)
    for step in range(sta_count - 1, 0, -1):
        peer = across(step)
        pl.semaphore_signal(barrier, inc=1, device_id=(days, peer, win), device_id_type=MESH)

    rows = 16
    lag = lax.broadcasted_iota(jnp.int32, (rows, LAGS), 1) - half
    sub = lax.broadcasted_iota(jnp.int32, (rows, LAGS), 0)

    @pl.loop(0, band // rows)
    def _(b):
        k = sub + (sta * band + b * rows)
        turn = ((k * lag + freq_bins) & (2 * freq_bins - 1)) - freq_bins
        c, s = cos_sin(turn.astype(jnp.float32) * (math.pi / freq_bins))
        at = pl.ds(pl.multiple_of(b * rows, rows), rows)
        lag_cos[at, :] = c.astype(jnp.bfloat16)
        lag_sin[at, :] = (-s).astype(jnp.bfloat16)

    for load in loads:
        load.wait()

    @pl.loop(0, win_rows)
    def _(w):
        weight = valid_ref[win * win_rows + w].astype(jnp.float32)
        c, s = cos_sin(phases_ref[w].astype(jnp.float32))
        cos_ref[w] = c.astype(jnp.bfloat16).astype(jnp.float32) * weight
        sin_ref[w] = s.astype(jnp.bfloat16).astype(jnp.float32) * weight

    count = valid_ref[0]
    for w in range(1, valid_ref.shape[0]):
        count = count + valid_ref[w]
    count = jnp.full((1, 128), count, jnp.int32).astype(jnp.float32)
    norm = 1.0 / jnp.sqrt(freq_bins * jnp.maximum(count, 1.0))
    lane_rows = band // 128
    weight = jnp.concatenate(
        [taper_ref[pl.ds(sta * lane_rows + r, 1), :] * norm for r in range(lane_rows)], axis=1
    )

    @pl.loop(0, stations // 2)
    def _(p):
        re = [jnp.zeros((stations, band), jnp.float32) for _ in range(2)]
        im = [jnp.zeros((stations, band), jnp.float32) for _ in range(2)]
        for w in range(win_rows):
            cj, sj = cos_ref[w], sin_ref[w]
            for q in range(2):
                ci = cos_ref[w, pl.ds(2 * p + q, 1), :]
                si = sin_ref[w, pl.ds(2 * p + q, 1), :]
                re[q] = re[q] + (ci * cj + si * sj)
                im[q] = im[q] + (si * cj - ci * sj)
        for q in range(2):
            at = pl.ds(pl.multiple_of((2 * p + q) * stations, stations), stations)
            spec_re[at, :] = (re[q] * weight).astype(jnp.bfloat16)
            spec_im[at, :] = (im[q] * weight).astype(jnp.bfloat16)

    def to_lags(which):
        at = pl.ds(pl.multiple_of(which * half, half), half)
        part = jnp.dot(spec_re[...], lag_cos[:, at], preferred_element_type=jnp.float32)
        return part + jnp.dot(spec_im[...], lag_sin[:, at], preferred_element_type=jnp.float32)

    other = to_lags(1 - win).astype(jnp.bfloat16)
    for b in range(sta_count):
        swap_out[b] = other[b * block : (b + 1) * block]
    pl.semaphore_wait(barrier, sta_count)

    def swap(step):
        peer = across(step)
        return pltpu.make_async_remote_copy(
            src_ref=swap_out.at[peer],
            dst_ref=swap_in.at[peer],
            send_sem=swap_send_sem.at[step],
            recv_sem=swap_recv_sem.at[step],
            device_id=(days, sta, 1 - win),
            device_id_type=MESH,
        )

    def scatter(step):
        peer = across(step)
        return pltpu.make_async_remote_copy(
            src_ref=send.at[peer],
            dst_ref=recv.at[step],
            send_sem=send_sem.at[step],
            recv_sem=recv_sem.at[step],
            device_id=(days, peer, win),
            device_id_type=MESH,
        )

    order = range(sta_count - 1, -1, -1)
    for step in order:
        swap(step).start()
    mine = to_lags(win)
    for b in range(sta_count):
        own[b] = mine[b * block : (b + 1) * block]
    for step in order:
        peer = across(step)
        swap(step).wait_recv()
        total = own[peer] + swap_in[peer].astype(jnp.float32)
        if step:
            send[peer] = total.astype(jnp.bfloat16)
            scatter(step).start()
    for step in range(1, sta_count):
        scatter(step).wait_recv()
        total = total + recv[step].astype(jnp.float32)

    source = lax.broadcasted_iota(jnp.int32, (stations, half), 0)
    keep = jnp.zeros((stations, half), jnp.float32)
    for b in range(sta_count):
        keep = jnp.where(source // recv_rows == b, mask_ref[sta, b].astype(jnp.float32), keep)
    for r in range(recv_rows):
        pair_keep = jnp.where(source == sta * recv_rows + r, 0.0, keep)
        out_ref[r] = total[r * stations : (r + 1) * stations] * pair_keep
    for step in order:
        swap(step).wait_send()
        if step:
            scatter(step).wait_send()


def fused(phases, window_valid, freq_taper, pair_mask):
    sta_count = lax.axis_size("sta")
    win_rows, band, stations = phases.shape
    recv_rows = stations // sta_count
    block = recv_rows * stations
    pairs = stations * stations
    half = LAGS // 2
    f32, bf16, vmem = jnp.float32, jnp.bfloat16, pltpu.VMEM
    return pl.pallas_call(
        lambda *refs: fused_kernel(*refs, sta_count=sta_count),
        name="fused",
        out_shape=jax.ShapeDtypeStruct((recv_rows, stations, half), f32),
        in_specs=[pl.BlockSpec(memory_space=pltpu.HBM)] * 4,
        out_specs=pl.BlockSpec(memory_space=pltpu.VMEM),
        scratch_shapes=[
            vmem((win_rows, stations, band), bf16),
            pltpu.SMEM(window_valid.shape, jnp.int32),
            vmem((freq_taper.shape[0] // 128, 128), f32),
            pltpu.SMEM(pair_mask.shape, jnp.int32),
            pltpu.SemaphoreType.DMA((4,)),
            vmem((win_rows, stations, band), f32),
            vmem((win_rows, stations, band), f32),
            vmem((pairs, band), bf16),
            vmem((pairs, band), bf16),
            vmem((band, LAGS), bf16),
            vmem((band, LAGS), bf16),
            vmem((sta_count, block, half), f32),
            vmem((sta_count, block, half), bf16),
            vmem((sta_count, block, half), bf16),
            vmem((sta_count, block, half), bf16),
            vmem((sta_count, block, half), bf16),
            pltpu.SemaphoreType.DMA((sta_count,)),
            pltpu.SemaphoreType.DMA((sta_count,)),
            pltpu.SemaphoreType.DMA((sta_count,)),
            pltpu.SemaphoreType.DMA((sta_count,)),
        ],
        compiler_params=pltpu.CompilerParams(
            collective_id=0, has_side_effects=True, vmem_limit_bytes=16 * 2**20
        ),
    )(
        *(
            pltpu.with_memory_space_constraint(a, pltpu.HBM)
            for a in (
                jnp.transpose(phases, (0, 2, 1)),
                window_valid,
                freq_taper.reshape(-1, 128),
                pair_mask,
            )
        )
    )


def lag_table(freq_bins, lag_count):
    freq_index = jnp.arange(freq_bins, dtype=jnp.int32)[:, None]
    lag_index = jnp.arange(lag_count, dtype=jnp.int32)[None, :] - lag_count // 2
    wrapped = jnp.mod(freq_index * lag_index, 2 * freq_bins)
    angle = wrapped.astype(jnp.float32) * (math.pi / freq_bins)
    return jnp.stack((jnp.cos(angle), -jnp.sin(angle))).astype(jnp.bfloat16)


def per_device(phases, window_valid, freq_taper, pair_mask):
    sta_count = lax.axis_size("sta")
    win_rows, band_bins, stations = phases.shape
    freq_bins = band_bins * sta_count
    recv_rows = stations // sta_count
    sta_index = lax.axis_index("sta")
    win_group = lax.axis_index("win")
    valid_count = jnp.sum(window_valid.astype(jnp.float32))
    norm_scale = 1.0 / jnp.sqrt(freq_bins * jnp.maximum(valid_count, 1.0))
    bin_weight = freq_taper * norm_scale
    group_valid = lax.dynamic_slice_in_dim(window_valid, win_group * win_rows, win_rows)
    group_weight = group_valid.astype(jnp.bfloat16)[:, None, None]
    own_f = phases.astype(jnp.float32)
    own_cos = jnp.cos(own_f).astype(jnp.bfloat16)
    own_sin = jnp.sin(own_f).astype(jnp.bfloat16)
    left_cos = own_cos * group_weight
    left_sin = own_sin * group_weight
    band_weight = lax.dynamic_slice_in_dim(bin_weight, sta_index * band_bins, band_bins)
    pair_re = jnp.einsum("wki,wkj->ijk", left_cos, own_cos, preferred_element_type=jnp.float32)
    pair_re = pair_re + jnp.einsum(
        "wki,wkj->ijk", left_sin, own_sin, preferred_element_type=jnp.float32
    )
    band_re = (pair_re * band_weight).astype(jnp.bfloat16)
    pair_im = jnp.einsum("wki,wkj->ijk", left_sin, own_cos, preferred_element_type=jnp.float32)
    pair_im = pair_im - jnp.einsum(
        "wki,wkj->ijk", left_cos, own_sin, preferred_element_type=jnp.float32
    )
    band_im = (pair_im * band_weight).astype(jnp.bfloat16)
    spectra = lax.all_to_all(
        jnp.stack((band_re, band_im)), "sta", split_axis=1, concat_axis=3, tiled=True
    )
    lag_count = LAGS
    transform = lag_table(freq_bins, lag_count)
    flat_spectra = spectra.reshape(2, recv_rows * stations, freq_bins)
    correlation = jnp.einsum(
        "cnk,ckt->nt", flat_spectra, transform, preferred_element_type=jnp.float32
    )
    block_row = lax.dynamic_index_in_dim(pair_mask, sta_index, 0, keepdims=False)
    station_row = jnp.repeat(block_row, recv_rows).astype(jnp.float32)
    receiver = sta_index * recv_rows + jnp.arange(recv_rows, dtype=jnp.int32)
    distinct = (receiver[:, None] != jnp.arange(stations, dtype=jnp.int32)[None, :]).astype(
        jnp.float32
    )
    pair_keep = station_row[None, :] * distinct
    correlation = correlation.reshape(recv_rows, stations, lag_count) * pair_keep[:, :, None]
    return lax.psum_scatter(correlation, "win", scatter_dimension=2, tiled=True)


def solution(mesh):
    def body(phases, window_valid, freq_taper, pair_mask):
        win_rows, band, stations = phases.shape
        sta_count, win_count = mesh.shape["sta"], mesh.shape["win"]
        power = band * sta_count & (band * sta_count - 1) == 0 and sta_count & (sta_count - 1) == 0
        if band % 128 == 0 and stations % 16 == 0 and win_count == 2 and power:
            return fused(phases, window_valid, freq_taper, pair_mask)
        return per_device(phases, window_valid, freq_taper, pair_mask)

    return jax.shard_map(
        body,
        mesh=mesh,
        in_specs=(P(("days", "win"), "sta", None), P("days"), P(), P()),
        out_specs=P(("days", "sta"), None, "win"),
        check_vma=False,
    )
```

```python
import math

import jax
import jax.numpy as jnp
import numpy as np
from jax import lax
from jax.experimental import pallas as pl
from jax.experimental.pallas import tpu as pltpu
from jax.sharding import PartitionSpec as P

LAGS = 512
MESH = pl.DeviceIdType.MESH


def fit(function, degree):
    nodes = np.polynomial.chebyshev.Chebyshev.interpolate(function, degree, domain=[0.0, math.pi**2])
    return [float(c) for c in nodes.convert(kind=np.polynomial.Polynomial).coef]


def sinc_of_square(y):
    x = np.sqrt(y)
    return np.sinc(x / math.pi)


SIN_COEF = fit(sinc_of_square, 7)
COS_COEF = fit(lambda y: np.cos(np.sqrt(y)), 8)


def horner(coef, y):
    total = jnp.full_like(y, coef[-1])
    for c in coef[-2::-1]:
        total = total * y + c
    return total


def cos_sin(x):
    y = x * x
    return horner(COS_COEF, y), x * horner(SIN_COEF, y)


def fused_kernel(
    phases_hbm,
    valid_hbm,
    taper_hbm,
    mask_hbm,
    out_ref,
    phases_ref,
    valid_ref,
    taper_ref,
    mask_ref,
    load_sem,
    cos_ref,
    sin_ref,
    spec_re,
    spec_im,
    lag_cos,
    lag_sin,
    own,
    swap_out,
    swap_in,
    send,
    recv,
    swap_send_sem,
    swap_recv_sem,
    send_sem,
    recv_sem,
    ready,
    *,
    sta_count,
):
    days, sta, win = (lax.axis_index(a) for a in ("days", "sta", "win"))
    win_rows, stations, band = phases_hbm.shape
    recv_rows = stations // sta_count
    block = recv_rows * stations
    freq_bins = band * sta_count
    half = LAGS // 2

    loads = [
        pltpu.make_async_copy(source, target, load_sem.at[n])
        for n, (source, target) in enumerate(
            (
                (phases_hbm, phases_ref),
                (valid_hbm, valid_ref),
                (taper_hbm, taper_ref),
                (mask_hbm, mask_ref),
            )
        )
    ]
    for load in loads:
        load.start()
    def across(step):
        bits = [2**n for n in range((sta_count - 1).bit_length())]
        return sum(lax.rem(lax.div(sta, n) + lax.div(jnp.int32(step), n), 2) * n for n in bits)

    barrier = pltpu.get_barrier_semaphore()
    for step in range(sta_count - 1, 0, -1):
        pl.semaphore_signal(barrier, inc=1, device_id=(days, across(step), 1), device_id_type=MESH)

    @pl.when(win == 1)
    def _():
        pl.semaphore_signal(barrier, inc=1, device_id=(days, sta, 0), device_id_type=MESH)

    rows = 16
    lag = lax.broadcasted_iota(jnp.int32, (rows, LAGS), 1) - half
    sub = lax.broadcasted_iota(jnp.int32, (rows, LAGS), 0)

    @pl.loop(0, band // rows)
    def _(b):
        k = sub + (sta * band + b * rows)
        turn = ((k * lag + freq_bins) & (2 * freq_bins - 1)) - freq_bins
        c, s = cos_sin(turn.astype(jnp.float32) * (math.pi / freq_bins))
        at = pl.ds(pl.multiple_of(b * rows, rows), rows)
        lag_cos[at, :] = c.astype(jnp.bfloat16)
        lag_sin[at, :] = (-s).astype(jnp.bfloat16)

    @pl.when(win == 0)
    def _():
        pl.semaphore_wait(barrier, 1)
        pl.semaphore_signal(ready, inc=1, device_id=(days, sta, 1), device_id_type=MESH)

    for load in loads:
        load.wait()

    @pl.loop(0, win_rows)
    def _(w):
        weight = valid_ref[win * win_rows + w].astype(jnp.float32)
        c, s = cos_sin(phases_ref[w].astype(jnp.float32))
        cos_ref[w] = c.astype(jnp.bfloat16).astype(jnp.float32) * weight
        sin_ref[w] = s.astype(jnp.bfloat16).astype(jnp.float32) * weight

    count = valid_ref[0]
    for w in range(1, valid_ref.shape[0]):
        count = count + valid_ref[w]
    count = jnp.full((1, 128), count, jnp.int32).astype(jnp.float32)
    norm = 1.0 / jnp.sqrt(freq_bins * jnp.maximum(count, 1.0))
    lane_rows = band // 128
    weight = jnp.concatenate(
        [taper_ref[pl.ds(sta * lane_rows + r, 1), :] * norm for r in range(lane_rows)], axis=1
    )

    def swap(step):
        return pltpu.make_async_remote_copy(
            src_ref=swap_out.at[step],
            dst_ref=swap_in.at[step],
            send_sem=swap_send_sem.at[step],
            recv_sem=swap_recv_sem.at[step],
            device_id=(days, sta, 1 - win),
            device_id_type=MESH,
        )

    def scatter(step):
        peer = across(step)
        return pltpu.make_async_remote_copy(
            src_ref=send.at[peer],
            dst_ref=recv.at[step],
            send_sem=send_sem.at[step],
            recv_sem=recv_sem.at[step],
            device_id=(days, peer, win),
            device_id_type=MESH,
        )

    def cross(step):
        first = across(step) * recv_rows
        re = [jnp.zeros((stations, band), jnp.float32) for _ in range(recv_rows)]
        im = [jnp.zeros((stations, band), jnp.float32) for _ in range(recv_rows)]
        for w in range(win_rows):
            cj, sj = cos_ref[w], sin_ref[w]
            for q in range(recv_rows):
                ci = cos_ref[w, pl.ds(first + q, 1), :]
                si = sin_ref[w, pl.ds(first + q, 1), :]
                re[q] = re[q] + (ci * cj + si * sj)
                im[q] = im[q] + (si * cj - ci * sj)
        at = pl.ds(pl.multiple_of(first * stations, block), block)
        made = [
            jnp.concatenate([(x * weight).astype(jnp.bfloat16) for x in part], axis=0)
            for part in (re, im)
        ]
        spec_re[at, :], spec_im[at, :] = made
        return made

    def to_lags(re, im, which):
        at = pl.ds(pl.multiple_of(which * half, half), half)
        part = jnp.dot(re, lag_cos[:, at], preferred_element_type=jnp.float32)
        return part + jnp.dot(im, lag_sin[:, at], preferred_element_type=jnp.float32)

    def pack(step, re, im):
        swap_out[step] = to_lags(re, im, 1 - win).astype(jnp.bfloat16)

    @pl.when(win == 1)
    def _():
        pl.semaphore_wait(ready, 1)

    def chunk(n, before):
        step = sta_count - 1 - n
        pack(step + 1, *before)
        made = cross(step)
        swap(step + 1).start()
        return made

    pack(0, *lax.fori_loop(1, sta_count, chunk, cross(sta_count - 1)))
    mine = to_lags(spec_re[...], spec_im[...], win)
    swap(0).start()
    order = range(sta_count - 1, -1, -1)
    for b in range(sta_count):
        own[b] = mine[b * block : (b + 1) * block]

    @pl.when(win == 1)
    def _():
        pl.semaphore_wait(barrier, 2 * (sta_count - 1))
        pl.semaphore_signal(ready, inc=1, device_id=(days, sta, 0), device_id_type=MESH)

    @pl.when(win == 0)
    def _():
        pl.semaphore_wait(ready, 1)

    for step in order:
        peer = across(step)
        swap(step).wait_recv()
        total = own[peer] + swap_in[step].astype(jnp.float32)
        if step:
            send[peer] = total.astype(jnp.bfloat16)
            scatter(step).start()
    for step in range(1, sta_count):
        scatter(step).wait_recv()
        total = total + recv[step].astype(jnp.float32)

    source = lax.broadcasted_iota(jnp.int32, (stations, half), 0)
    keep = jnp.zeros((stations, half), jnp.float32)
    for b in range(sta_count):
        keep = jnp.where(source // recv_rows == b, mask_ref[sta, b].astype(jnp.float32), keep)
    for r in range(recv_rows):
        pair_keep = jnp.where(source == sta * recv_rows + r, 0.0, keep)
        out_ref[r] = total[r * stations : (r + 1) * stations] * pair_keep
    for step in order:
        swap(step).wait_send()
        if step:
            scatter(step).wait_send()


def fused(phases, window_valid, freq_taper, pair_mask):
    sta_count = lax.axis_size("sta")
    win_rows, band, stations = phases.shape
    recv_rows = stations // sta_count
    block = recv_rows * stations
    pairs = stations * stations
    half = LAGS // 2
    f32, bf16, vmem = jnp.float32, jnp.bfloat16, pltpu.VMEM
    return pl.pallas_call(
        lambda *refs: fused_kernel(*refs, sta_count=sta_count),
        name="fused",
        out_shape=jax.ShapeDtypeStruct((recv_rows, stations, half), f32),
        in_specs=[pl.BlockSpec(memory_space=pltpu.HBM)] * 4,
        out_specs=pl.BlockSpec(memory_space=pltpu.VMEM),
        scratch_shapes=[
            vmem((win_rows, stations, band), bf16),
            pltpu.SMEM(window_valid.shape, jnp.int32),
            vmem((freq_taper.shape[0] // 128, 128), f32),
            pltpu.SMEM(pair_mask.shape, jnp.int32),
            pltpu.SemaphoreType.DMA((4,)),
            vmem((win_rows, stations, band), f32),
            vmem((win_rows, stations, band), f32),
            vmem((pairs, band), bf16),
            vmem((pairs, band), bf16),
            vmem((band, LAGS), bf16),
            vmem((band, LAGS), bf16),
            vmem((sta_count, block, half), f32),
            vmem((sta_count, block, half), bf16),
            vmem((sta_count, block, half), bf16),
            vmem((sta_count, block, half), bf16),
            vmem((sta_count, block, half), bf16),
            pltpu.SemaphoreType.DMA((sta_count,)),
            pltpu.SemaphoreType.DMA((sta_count,)),
            pltpu.SemaphoreType.DMA((sta_count,)),
            pltpu.SemaphoreType.DMA((sta_count,)),
            pltpu.SemaphoreType.REGULAR,
        ],
        compiler_params=pltpu.CompilerParams(
            collective_id=0, has_side_effects=True, vmem_limit_bytes=16 * 2**20
        ),
    )(
        *(
            pltpu.with_memory_space_constraint(a, pltpu.HBM)
            for a in (
                jnp.transpose(phases, (0, 2, 1)),
                window_valid,
                freq_taper.reshape(-1, 128),
                pair_mask,
            )
        )
    )


def lag_table(freq_bins, lag_count):
    freq_index = jnp.arange(freq_bins, dtype=jnp.int32)[:, None]
    lag_index = jnp.arange(lag_count, dtype=jnp.int32)[None, :] - lag_count // 2
    wrapped = jnp.mod(freq_index * lag_index, 2 * freq_bins)
    angle = wrapped.astype(jnp.float32) * (math.pi / freq_bins)
    return jnp.stack((jnp.cos(angle), -jnp.sin(angle))).astype(jnp.bfloat16)


def per_device(phases, window_valid, freq_taper, pair_mask):
    sta_count = lax.axis_size("sta")
    win_rows, band_bins, stations = phases.shape
    freq_bins = band_bins * sta_count
    recv_rows = stations // sta_count
    sta_index = lax.axis_index("sta")
    win_group = lax.axis_index("win")
    valid_count = jnp.sum(window_valid.astype(jnp.float32))
    norm_scale = 1.0 / jnp.sqrt(freq_bins * jnp.maximum(valid_count, 1.0))
    bin_weight = freq_taper * norm_scale
    group_valid = lax.dynamic_slice_in_dim(window_valid, win_group * win_rows, win_rows)
    group_weight = group_valid.astype(jnp.bfloat16)[:, None, None]
    own_f = phases.astype(jnp.float32)
    own_cos = jnp.cos(own_f).astype(jnp.bfloat16)
    own_sin = jnp.sin(own_f).astype(jnp.bfloat16)
    left_cos = own_cos * group_weight
    left_sin = own_sin * group_weight
    band_weight = lax.dynamic_slice_in_dim(bin_weight, sta_index * band_bins, band_bins)
    pair_re = jnp.einsum("wki,wkj->ijk", left_cos, own_cos, preferred_element_type=jnp.float32)
    pair_re = pair_re + jnp.einsum(
        "wki,wkj->ijk", left_sin, own_sin, preferred_element_type=jnp.float32
    )
    band_re = (pair_re * band_weight).astype(jnp.bfloat16)
    pair_im = jnp.einsum("wki,wkj->ijk", left_sin, own_cos, preferred_element_type=jnp.float32)
    pair_im = pair_im - jnp.einsum(
        "wki,wkj->ijk", left_cos, own_sin, preferred_element_type=jnp.float32
    )
    band_im = (pair_im * band_weight).astype(jnp.bfloat16)
    spectra = lax.all_to_all(
        jnp.stack((band_re, band_im)), "sta", split_axis=1, concat_axis=3, tiled=True
    )
    lag_count = LAGS
    transform = lag_table(freq_bins, lag_count)
    flat_spectra = spectra.reshape(2, recv_rows * stations, freq_bins)
    correlation = jnp.einsum(
        "cnk,ckt->nt", flat_spectra, transform, preferred_element_type=jnp.float32
    )
    block_row = lax.dynamic_index_in_dim(pair_mask, sta_index, 0, keepdims=False)
    station_row = jnp.repeat(block_row, recv_rows).astype(jnp.float32)
    receiver = sta_index * recv_rows + jnp.arange(recv_rows, dtype=jnp.int32)
    distinct = (receiver[:, None] != jnp.arange(stations, dtype=jnp.int32)[None, :]).astype(
        jnp.float32
    )
    pair_keep = station_row[None, :] * distinct
    correlation = correlation.reshape(recv_rows, stations, lag_count) * pair_keep[:, :, None]
    return lax.psum_scatter(correlation, "win", scatter_dimension=2, tiled=True)


def solution(mesh):
    def body(phases, window_valid, freq_taper, pair_mask):
        win_rows, band, stations = phases.shape
        sta_count, win_count = mesh.shape["sta"], mesh.shape["win"]
        power = band * sta_count & (band * sta_count - 1) == 0 and sta_count & (sta_count - 1) == 0
        if band % 128 == 0 and stations % 16 == 0 and win_count == 2 and power:
            return fused(phases, window_valid, freq_taper, pair_mask)
        return per_device(phases, window_valid, freq_taper, pair_mask)

    return jax.shard_map(
        body,
        mesh=mesh,
        in_specs=(P(("days", "win"), "sta", None), P("days"), P(), P()),
        out_specs=P(("days", "sta"), None, "win"),
        check_vma=False,
    )
```

```python
import math

import jax
import jax.numpy as jnp
import numpy as np
from jax import lax
from jax.experimental import pallas as pl
from jax.experimental.pallas import tpu as pltpu
from jax.sharding import PartitionSpec as P

LAGS = 512
MESH = pl.DeviceIdType.MESH


def fit(function, degree):
    nodes = np.polynomial.chebyshev.Chebyshev.interpolate(function, degree, domain=[0.0, math.pi**2])
    return [float(c) for c in nodes.convert(kind=np.polynomial.Polynomial).coef]


def sinc_of_square(y):
    x = np.sqrt(y)
    return np.sinc(x / math.pi)


SIN_COEF = fit(sinc_of_square, 7)
COS_COEF = fit(lambda y: np.cos(np.sqrt(y)), 8)


def horner(coef, y):
    total = jnp.full_like(y, coef[-1])
    for c in coef[-2::-1]:
        total = total * y + c
    return total


def cos_sin(x):
    y = x * x
    return horner(COS_COEF, y), x * horner(SIN_COEF, y)


def fused_kernel(
    phases_hbm,
    valid_hbm,
    taper_hbm,
    mask_hbm,
    out_ref,
    phases_ref,
    valid_ref,
    taper_ref,
    mask_ref,
    load_sem,
    cos_ref,
    sin_ref,
    spec_re,
    spec_im,
    lag_cos,
    lag_sin,
    own,
    swap_out,
    swap_in,
    send,
    recv,
    beside_out,
    beside_in,
    beside_send_sem,
    beside_recv_sem,
    swap_send_sem,
    swap_recv_sem,
    send_sem,
    recv_sem,
    ready,
    *,
    sta_count,
):
    days, sta, win = (lax.axis_index(a) for a in ("days", "sta", "win"))
    win_rows, stations, band = phases_hbm.shape
    recv_rows = stations // sta_count
    block = recv_rows * stations
    freq_bins = band * sta_count
    half = LAGS // 2

    loads = [
        pltpu.make_async_copy(source, target, load_sem.at[n])
        for n, (source, target) in enumerate(
            (
                (phases_hbm, phases_ref),
                (valid_hbm, valid_ref),
                (taper_hbm, taper_ref),
                (mask_hbm, mask_ref),
            )
        )
    ]
    for load in loads:
        load.start()
    def across(step):
        bits = [2**n for n in range((sta_count - 1).bit_length())]
        return sum(lax.rem(lax.div(sta, n) + lax.div(jnp.int32(step), n), 2) * n for n in bits)

    barrier = pltpu.get_barrier_semaphore()
    for step in range(sta_count - 1, 0, -1):
        pl.semaphore_signal(
            barrier, inc=1, device_id=(days, across(step), int(step > 1)), device_id_type=MESH
        )

    @pl.when(win == 1)
    def _():
        pl.semaphore_signal(barrier, inc=1, device_id=(days, sta, 0), device_id_type=MESH)

    rows = 16
    lag = lax.broadcasted_iota(jnp.int32, (rows, LAGS), 1) - half
    sub = lax.broadcasted_iota(jnp.int32, (rows, LAGS), 0)

    @pl.loop(0, band // rows)
    def _(b):
        k = sub + (sta * band + b * rows)
        turn = ((k * lag + freq_bins) & (2 * freq_bins - 1)) - freq_bins
        c, s = cos_sin(turn.astype(jnp.float32) * (math.pi / freq_bins))
        at = pl.ds(pl.multiple_of(b * rows, rows), rows)
        lag_cos[at, :] = c.astype(jnp.bfloat16)
        lag_sin[at, :] = (-s).astype(jnp.bfloat16)

    @pl.when(win == 0)
    def _():
        pl.semaphore_wait(barrier, 3)
        pl.semaphore_signal(ready, inc=1, device_id=(days, sta, 1), device_id_type=MESH)

    for load in loads:
        load.wait()

    @pl.loop(0, win_rows)
    def _(w):
        weight = valid_ref[win * win_rows + w].astype(jnp.float32)
        c, s = cos_sin(phases_ref[w].astype(jnp.float32))
        cos_ref[w] = c.astype(jnp.bfloat16).astype(jnp.float32) * weight
        sin_ref[w] = s.astype(jnp.bfloat16).astype(jnp.float32) * weight

    count = valid_ref[0]
    for w in range(1, valid_ref.shape[0]):
        count = count + valid_ref[w]
    count = jnp.full((1, 128), count, jnp.int32).astype(jnp.float32)
    norm = 1.0 / jnp.sqrt(freq_bins * jnp.maximum(count, 1.0))
    lane_rows = band // 128
    weight = jnp.concatenate(
        [taper_ref[pl.ds(sta * lane_rows + r, 1), :] * norm for r in range(lane_rows)], axis=1
    )

    def swap(step):
        return pltpu.make_async_remote_copy(
            src_ref=swap_out.at[step],
            dst_ref=swap_in.at[step],
            send_sem=swap_send_sem.at[step],
            recv_sem=swap_recv_sem.at[step],
            device_id=(days, sta, 1 - win),
            device_id_type=MESH,
        )

    def scatter(step):
        peer = across(step)
        return pltpu.make_async_remote_copy(
            src_ref=send.at[peer],
            dst_ref=recv.at[step],
            send_sem=send_sem.at[step],
            recv_sem=recv_sem.at[step],
            device_id=(days, peer, win),
            device_id_type=MESH,
        )

    def beside(slot):
        return pltpu.make_async_remote_copy(
            src_ref=beside_out.at[slot],
            dst_ref=beside_in.at[slot],
            send_sem=beside_send_sem.at[slot],
            recv_sem=beside_recv_sem.at[slot],
            device_id=(days, across(1), win),
            device_id_type=MESH,
        )

    def cross(step):
        first = across(step) * recv_rows
        re = [jnp.zeros((stations, band), jnp.float32) for _ in range(recv_rows)]
        im = [jnp.zeros((stations, band), jnp.float32) for _ in range(recv_rows)]
        for w in range(win_rows):
            cj, sj = cos_ref[w], sin_ref[w]
            for q in range(recv_rows):
                ci = cos_ref[w, pl.ds(first + q, 1), :]
                si = sin_ref[w, pl.ds(first + q, 1), :]
                re[q] = re[q] + (ci * cj + si * sj)
                im[q] = im[q] + (si * cj - ci * sj)
        at = pl.ds(pl.multiple_of(first * stations, block), block)
        made = [
            jnp.concatenate([(x * weight).astype(jnp.bfloat16) for x in part], axis=0)
            for part in (re, im)
        ]
        spec_re[at, :], spec_im[at, :] = made
        return made

    def to_lags(re, im, which):
        at = pl.ds(pl.multiple_of(which * half, half), half)
        part = jnp.dot(re, lag_cos[:, at], preferred_element_type=jnp.float32)
        return part + jnp.dot(im, lag_sin[:, at], preferred_element_type=jnp.float32)

    def pack(step, re, im):
        swap_out[step] = to_lags(re, im, 1 - win).astype(jnp.bfloat16)

    @pl.when(win == 1)
    def _():
        pl.semaphore_wait(ready, 1)

    def chunk(n, before):
        step = sta_count - 1 - n
        pack(step + 1, *before)
        made = cross(step)
        swap(step + 1).start()
        return made

    pack(0, *lax.fori_loop(1, sta_count, chunk, cross(sta_count - 1)))
    mine = to_lags(spec_re[...], spec_im[...], win)
    swap(0).start()
    for b in range(sta_count):
        own[b] = mine[b * block : (b + 1) * block]

    def over_groups(step):
        swap(step).wait_recv()
        return own[across(step)] + swap_in[step].astype(jnp.float32)

    for slot, step in enumerate((7, 5)):
        beside_out[slot] = over_groups(step).astype(jnp.bfloat16)
        beside(slot).start()
    far = [over_groups(step) for step in (6, 4)]
    for step in (1, 3, 2):
        send[across(step)] = over_groups(step).astype(jnp.bfloat16)
    scatter(1).start()
    total = over_groups(0)

    @pl.when(win == 1)
    def _():
        pl.semaphore_wait(barrier, 2 * (sta_count - 2))
        pl.semaphore_signal(ready, inc=1, device_id=(days, sta, 0), device_id_type=MESH)

    @pl.when(win == 0)
    def _():
        pl.semaphore_wait(ready, 1)

    for slot, step in enumerate((6, 4)):
        beside(slot).wait_recv()
        chunk_sum = far[slot] + beside_in[slot].astype(jnp.float32)
        send[across(step)] = chunk_sum.astype(jnp.bfloat16)
        scatter(step).start()
    for step in (3, 2):
        scatter(step).start()
    sent = (1, 2, 3, 4, 6)
    for step in sent:
        scatter(step).wait_recv()
        total = total + recv[step].astype(jnp.float32)

    source = lax.broadcasted_iota(jnp.int32, (stations, half), 0)
    keep = jnp.zeros((stations, half), jnp.float32)
    for b in range(sta_count):
        keep = jnp.where(source // recv_rows == b, mask_ref[sta, b].astype(jnp.float32), keep)
    for r in range(recv_rows):
        pair_keep = jnp.where(source == sta * recv_rows + r, 0.0, keep)
        out_ref[r] = total[r * stations : (r + 1) * stations] * pair_keep
    for step in range(sta_count):
        swap(step).wait_send()
    for slot in range(2):
        beside(slot).wait_send()
    for step in sent:
        scatter(step).wait_send()


def fused(phases, window_valid, freq_taper, pair_mask):
    sta_count = lax.axis_size("sta")
    win_rows, band, stations = phases.shape
    recv_rows = stations // sta_count
    block = recv_rows * stations
    pairs = stations * stations
    half = LAGS // 2
    f32, bf16, vmem = jnp.float32, jnp.bfloat16, pltpu.VMEM
    return pl.pallas_call(
        lambda *refs: fused_kernel(*refs, sta_count=sta_count),
        name="fused",
        out_shape=jax.ShapeDtypeStruct((recv_rows, stations, half), f32),
        in_specs=[pl.BlockSpec(memory_space=pltpu.HBM)] * 4,
        out_specs=pl.BlockSpec(memory_space=pltpu.VMEM),
        scratch_shapes=[
            vmem((win_rows, stations, band), bf16),
            pltpu.SMEM(window_valid.shape, jnp.int32),
            vmem((freq_taper.shape[0] // 128, 128), f32),
            pltpu.SMEM(pair_mask.shape, jnp.int32),
            pltpu.SemaphoreType.DMA((4,)),
            vmem((win_rows, stations, band), f32),
            vmem((win_rows, stations, band), f32),
            vmem((pairs, band), bf16),
            vmem((pairs, band), bf16),
            vmem((band, LAGS), bf16),
            vmem((band, LAGS), bf16),
            vmem((sta_count, block, half), f32),
            vmem((sta_count, block, half), bf16),
            vmem((sta_count, block, half), bf16),
            vmem((sta_count, block, half), bf16),
            vmem((sta_count, block, half), bf16),
            vmem((2, block, half), bf16),
            vmem((2, block, half), bf16),
            pltpu.SemaphoreType.DMA((2,)),
            pltpu.SemaphoreType.DMA((2,)),
            pltpu.SemaphoreType.DMA((sta_count,)),
            pltpu.SemaphoreType.DMA((sta_count,)),
            pltpu.SemaphoreType.DMA((sta_count,)),
            pltpu.SemaphoreType.DMA((sta_count,)),
            pltpu.SemaphoreType.REGULAR,
        ],
        compiler_params=pltpu.CompilerParams(
            collective_id=0, has_side_effects=True, vmem_limit_bytes=16 * 2**20
        ),
    )(
        *(
            pltpu.with_memory_space_constraint(a, pltpu.HBM)
            for a in (
                jnp.transpose(phases, (0, 2, 1)),
                window_valid,
                freq_taper.reshape(-1, 128),
                pair_mask,
            )
        )
    )


def lag_table(freq_bins, lag_count):
    freq_index = jnp.arange(freq_bins, dtype=jnp.int32)[:, None]
    lag_index = jnp.arange(lag_count, dtype=jnp.int32)[None, :] - lag_count // 2
    wrapped = jnp.mod(freq_index * lag_index, 2 * freq_bins)
    angle = wrapped.astype(jnp.float32) * (math.pi / freq_bins)
    return jnp.stack((jnp.cos(angle), -jnp.sin(angle))).astype(jnp.bfloat16)


def per_device(phases, window_valid, freq_taper, pair_mask):
    sta_count = lax.axis_size("sta")
    win_rows, band_bins, stations = phases.shape
    freq_bins = band_bins * sta_count
    recv_rows = stations // sta_count
    sta_index = lax.axis_index("sta")
    win_group = lax.axis_index("win")
    valid_count = jnp.sum(window_valid.astype(jnp.float32))
    norm_scale = 1.0 / jnp.sqrt(freq_bins * jnp.maximum(valid_count, 1.0))
    bin_weight = freq_taper * norm_scale
    group_valid = lax.dynamic_slice_in_dim(window_valid, win_group * win_rows, win_rows)
    group_weight = group_valid.astype(jnp.bfloat16)[:, None, None]
    own_f = phases.astype(jnp.float32)
    own_cos = jnp.cos(own_f).astype(jnp.bfloat16)
    own_sin = jnp.sin(own_f).astype(jnp.bfloat16)
    left_cos = own_cos * group_weight
    left_sin = own_sin * group_weight
    band_weight = lax.dynamic_slice_in_dim(bin_weight, sta_index * band_bins, band_bins)
    pair_re = jnp.einsum("wki,wkj->ijk", left_cos, own_cos, preferred_element_type=jnp.float32)
    pair_re = pair_re + jnp.einsum(
        "wki,wkj->ijk", left_sin, own_sin, preferred_element_type=jnp.float32
    )
    band_re = (pair_re * band_weight).astype(jnp.bfloat16)
    pair_im = jnp.einsum("wki,wkj->ijk", left_sin, own_cos, preferred_element_type=jnp.float32)
    pair_im = pair_im - jnp.einsum(
        "wki,wkj->ijk", left_cos, own_sin, preferred_element_type=jnp.float32
    )
    band_im = (pair_im * band_weight).astype(jnp.bfloat16)
    spectra = lax.all_to_all(
        jnp.stack((band_re, band_im)), "sta", split_axis=1, concat_axis=3, tiled=True
    )
    lag_count = LAGS
    transform = lag_table(freq_bins, lag_count)
    flat_spectra = spectra.reshape(2, recv_rows * stations, freq_bins)
    correlation = jnp.einsum(
        "cnk,ckt->nt", flat_spectra, transform, preferred_element_type=jnp.float32
    )
    block_row = lax.dynamic_index_in_dim(pair_mask, sta_index, 0, keepdims=False)
    station_row = jnp.repeat(block_row, recv_rows).astype(jnp.float32)
    receiver = sta_index * recv_rows + jnp.arange(recv_rows, dtype=jnp.int32)
    distinct = (receiver[:, None] != jnp.arange(stations, dtype=jnp.int32)[None, :]).astype(
        jnp.float32
    )
    pair_keep = station_row[None, :] * distinct
    correlation = correlation.reshape(recv_rows, stations, lag_count) * pair_keep[:, :, None]
    return lax.psum_scatter(correlation, "win", scatter_dimension=2, tiled=True)


def solution(mesh):
    def body(phases, window_valid, freq_taper, pair_mask):
        win_rows, band, stations = phases.shape
        sta_count, win_count = mesh.shape["sta"], mesh.shape["win"]
        power = band * sta_count & (band * sta_count - 1) == 0
        if sta_count == 8 and band % 128 == 0 and stations % 16 == 0 and win_count == 2 and power:
            return fused(phases, window_valid, freq_taper, pair_mask)
        return per_device(phases, window_valid, freq_taper, pair_mask)

    return jax.shard_map(
        body,
        mesh=mesh,
        in_specs=(P(("days", "win"), "sta", None), P("days"), P(), P()),
        out_specs=P(("days", "sta"), None, "win"),
        check_vma=False,
    )
```

```python
import math

import jax
import jax.numpy as jnp
import numpy as np
from jax import lax
from jax.experimental import pallas as pl
from jax.experimental.pallas import tpu as pltpu
from jax.sharding import PartitionSpec as P

LAGS = 512
MESH = pl.DeviceIdType.MESH


def fit(function, degree):
    nodes = np.polynomial.chebyshev.Chebyshev.interpolate(function, degree, domain=[0.0, math.pi**2])
    return [float(c) for c in nodes.convert(kind=np.polynomial.Polynomial).coef]


def sinc_of_square(y):
    x = np.sqrt(y)
    return np.sinc(x / math.pi)


SIN_COEF = fit(sinc_of_square, 7)
COS_COEF = fit(lambda y: np.cos(np.sqrt(y)), 8)


def horner(coef, y):
    total = jnp.full_like(y, coef[-1])
    for c in coef[-2::-1]:
        total = total * y + c
    return total


def cos_sin(x):
    y = x * x
    return horner(COS_COEF, y), x * horner(SIN_COEF, y)


def fused_kernel(
    phases_hbm,
    valid_hbm,
    taper_hbm,
    mask_hbm,
    out_ref,
    phases_ref,
    valid_ref,
    taper_ref,
    mask_ref,
    load_sem,
    cos_ref,
    sin_ref,
    spec_re,
    spec_im,
    lag_cos,
    lag_sin,
    own,
    swap_out,
    swap_in,
    send,
    recv,
    swap_send_sem,
    swap_recv_sem,
    send_sem,
    recv_sem,
    ready,
    *,
    sta_count,
):
    days, sta, win = (lax.axis_index(a) for a in ("days", "sta", "win"))
    win_rows, stations, band = phases_hbm.shape
    recv_rows = stations // sta_count
    block = recv_rows * stations
    freq_bins = band * sta_count
    half = LAGS // 2

    loads = [
        pltpu.make_async_copy(source, target, load_sem.at[n])
        for n, (source, target) in enumerate(
            (
                (phases_hbm, phases_ref),
                (valid_hbm, valid_ref),
                (taper_hbm, taper_ref),
                (mask_hbm, mask_ref),
            )
        )
    ]
    for load in loads:
        load.start()
    def across(step):
        bits = [2**n for n in range((sta_count - 1).bit_length())]
        flips = bits[1::-1] + bits[2:]
        return sum(
            lax.rem(lax.div(sta, n) + lax.div(jnp.int32(step), m), 2) * n
            for n, m in zip(bits, flips)
        )

    barrier = pltpu.get_barrier_semaphore()
    for step in range(sta_count - 1, 0, -1):
        pl.semaphore_signal(barrier, inc=1, device_id=(days, across(step), 1), device_id_type=MESH)

    @pl.when(win == 1)
    def _():
        pl.semaphore_signal(barrier, inc=1, device_id=(days, sta, 0), device_id_type=MESH)

    rows = 16
    lag = lax.broadcasted_iota(jnp.int32, (rows, LAGS), 1) - half
    sub = lax.broadcasted_iota(jnp.int32, (rows, LAGS), 0)

    @pl.loop(0, band // rows)
    def _(b):
        k = sub + (sta * band + b * rows)
        turn = ((k * lag + freq_bins) & (2 * freq_bins - 1)) - freq_bins
        c, s = cos_sin(turn.astype(jnp.float32) * (math.pi / freq_bins))
        at = pl.ds(pl.multiple_of(b * rows, rows), rows)
        lag_cos[at, :] = c.astype(jnp.bfloat16)
        lag_sin[at, :] = (-s).astype(jnp.bfloat16)

    @pl.when(win == 0)
    def _():
        pl.semaphore_wait(barrier, 1)
        pl.semaphore_signal(ready, inc=1, device_id=(days, sta, 1), device_id_type=MESH)

    for load in loads:
        load.wait()

    for w in range(win_rows):
        weight = valid_ref[win * win_rows + w].astype(jnp.float32)
        c, s = cos_sin(phases_ref[w].astype(jnp.float32))
        cos_ref[w] = c.astype(jnp.bfloat16).astype(jnp.float32) * weight
        sin_ref[w] = s.astype(jnp.bfloat16).astype(jnp.float32) * weight

    count = valid_ref[0]
    for w in range(1, valid_ref.shape[0]):
        count = count + valid_ref[w]
    count = jnp.full((1, 128), count, jnp.int32).astype(jnp.float32)
    norm = 1.0 / jnp.sqrt(freq_bins * jnp.maximum(count, 1.0))
    lane_rows = band // 128
    weight = jnp.concatenate(
        [taper_ref[pl.ds(sta * lane_rows + r, 1), :] * norm for r in range(lane_rows)], axis=1
    )

    def swap(step):
        return pltpu.make_async_remote_copy(
            src_ref=swap_out.at[step],
            dst_ref=swap_in.at[step],
            send_sem=swap_send_sem.at[step],
            recv_sem=swap_recv_sem.at[step],
            device_id=(days, sta, 1 - win),
            device_id_type=MESH,
        )

    def scatter(step):
        peer = across(step)
        return pltpu.make_async_remote_copy(
            src_ref=send.at[peer],
            dst_ref=recv.at[step],
            send_sem=send_sem.at[step],
            recv_sem=recv_sem.at[step],
            device_id=(days, peer, win),
            device_id_type=MESH,
        )

    def cross(step):
        first = across(step) * recv_rows
        re = [jnp.zeros((stations, band), jnp.float32) for _ in range(recv_rows)]
        im = [jnp.zeros((stations, band), jnp.float32) for _ in range(recv_rows)]
        for w in range(win_rows):
            cj, sj = cos_ref[w], sin_ref[w]
            for q in range(recv_rows):
                ci = cos_ref[w, pl.ds(first + q, 1), :]
                si = sin_ref[w, pl.ds(first + q, 1), :]
                re[q] = re[q] + (ci * cj + si * sj)
                im[q] = im[q] + (si * cj - ci * sj)
        at = pl.ds(pl.multiple_of(first * stations, block), block)
        made = [
            jnp.concatenate([(x * weight).astype(jnp.bfloat16) for x in part], axis=0)
            for part in (re, im)
        ]
        spec_re[at, :], spec_im[at, :] = made
        return made

    def to_lags(re, im, which):
        at = pl.ds(pl.multiple_of(which * half, half), half)
        part = jnp.dot(re, lag_cos[:, at], preferred_element_type=jnp.float32)
        return part + jnp.dot(im, lag_sin[:, at], preferred_element_type=jnp.float32)

    def pack(step, re, im):
        swap_out[step] = to_lags(re, im, 1 - win).astype(jnp.bfloat16)

    @pl.when(win == 1)
    def _():
        pl.semaphore_wait(ready, 1)

    def chunk(n, before):
        step = sta_count - 1 - n
        pack(step + 1, *before)
        made = cross(step)
        swap(step + 1).start()
        return made

    pack(0, *lax.fori_loop(1, sta_count, chunk, cross(sta_count - 1)))
    mine = to_lags(spec_re[...], spec_im[...], win)
    swap(0).start()
    order = range(sta_count - 1, -1, -1)
    for b in range(sta_count):
        own[b] = mine[b * block : (b + 1) * block]

    @pl.when(win == 1)
    def _():
        pl.semaphore_wait(barrier, 2 * (sta_count - 1))
        pl.semaphore_signal(ready, inc=1, device_id=(days, sta, 0), device_id_type=MESH)

    @pl.when(win == 0)
    def _():
        pl.semaphore_wait(ready, 1)

    for step in order:
        peer = across(step)
        swap(step).wait_recv()
        total = own[peer] + swap_in[step].astype(jnp.float32)
        if step:
            send[peer] = total.astype(jnp.bfloat16)
            scatter(step).start()
    for step in range(1, sta_count):
        scatter(step).wait_recv()
        total = total + recv[step].astype(jnp.float32)

    source = lax.broadcasted_iota(jnp.int32, (stations, half), 0)
    keep = jnp.zeros((stations, half), jnp.float32)
    for b in range(sta_count):
        keep = jnp.where(source // recv_rows == b, mask_ref[sta, b].astype(jnp.float32), keep)
    for r in range(recv_rows):
        pair_keep = jnp.where(source == sta * recv_rows + r, 0.0, keep)
        out_ref[r] = total[r * stations : (r + 1) * stations] * pair_keep
    for step in order:
        swap(step).wait_send()
        if step:
            scatter(step).wait_send()


def fused(phases, window_valid, freq_taper, pair_mask):
    sta_count = lax.axis_size("sta")
    win_rows, band, stations = phases.shape
    recv_rows = stations // sta_count
    block = recv_rows * stations
    pairs = stations * stations
    half = LAGS // 2
    f32, bf16, vmem = jnp.float32, jnp.bfloat16, pltpu.VMEM
    return pl.pallas_call(
        lambda *refs: fused_kernel(*refs, sta_count=sta_count),
        name="fused",
        out_shape=jax.ShapeDtypeStruct((recv_rows, stations, half), f32),
        in_specs=[pl.BlockSpec(memory_space=pltpu.HBM)] * 4,
        out_specs=pl.BlockSpec(memory_space=pltpu.VMEM),
        scratch_shapes=[
            vmem((win_rows, stations, band), bf16),
            pltpu.SMEM(window_valid.shape, jnp.int32),
            vmem((freq_taper.shape[0] // 128, 128), f32),
            pltpu.SMEM(pair_mask.shape, jnp.int32),
            pltpu.SemaphoreType.DMA((4,)),
            vmem((win_rows, stations, band), f32),
            vmem((win_rows, stations, band), f32),
            vmem((pairs, band), bf16),
            vmem((pairs, band), bf16),
            vmem((band, LAGS), bf16),
            vmem((band, LAGS), bf16),
            vmem((sta_count, block, half), f32),
            vmem((sta_count, block, half), bf16),
            vmem((sta_count, block, half), bf16),
            vmem((sta_count, block, half), bf16),
            vmem((sta_count, block, half), bf16),
            pltpu.SemaphoreType.DMA((sta_count,)),
            pltpu.SemaphoreType.DMA((sta_count,)),
            pltpu.SemaphoreType.DMA((sta_count,)),
            pltpu.SemaphoreType.DMA((sta_count,)),
            pltpu.SemaphoreType.REGULAR,
        ],
        compiler_params=pltpu.CompilerParams(
            collective_id=0, has_side_effects=True, vmem_limit_bytes=16 * 2**20
        ),
    )(
        *(
            pltpu.with_memory_space_constraint(a, pltpu.HBM)
            for a in (
                jnp.transpose(phases, (0, 2, 1)),
                window_valid,
                freq_taper.reshape(-1, 128),
                pair_mask,
            )
        )
    )


def lag_table(freq_bins, lag_count):
    freq_index = jnp.arange(freq_bins, dtype=jnp.int32)[:, None]
    lag_index = jnp.arange(lag_count, dtype=jnp.int32)[None, :] - lag_count // 2
    wrapped = jnp.mod(freq_index * lag_index, 2 * freq_bins)
    angle = wrapped.astype(jnp.float32) * (math.pi / freq_bins)
    return jnp.stack((jnp.cos(angle), -jnp.sin(angle))).astype(jnp.bfloat16)


def per_device(phases, window_valid, freq_taper, pair_mask):
    sta_count = lax.axis_size("sta")
    win_rows, band_bins, stations = phases.shape
    freq_bins = band_bins * sta_count
    recv_rows = stations // sta_count
    sta_index = lax.axis_index("sta")
    win_group = lax.axis_index("win")
    valid_count = jnp.sum(window_valid.astype(jnp.float32))
    norm_scale = 1.0 / jnp.sqrt(freq_bins * jnp.maximum(valid_count, 1.0))
    bin_weight = freq_taper * norm_scale
    group_valid = lax.dynamic_slice_in_dim(window_valid, win_group * win_rows, win_rows)
    group_weight = group_valid.astype(jnp.bfloat16)[:, None, None]
    own_f = phases.astype(jnp.float32)
    own_cos = jnp.cos(own_f).astype(jnp.bfloat16)
    own_sin = jnp.sin(own_f).astype(jnp.bfloat16)
    left_cos = own_cos * group_weight
    left_sin = own_sin * group_weight
    band_weight = lax.dynamic_slice_in_dim(bin_weight, sta_index * band_bins, band_bins)
    pair_re = jnp.einsum("wki,wkj->ijk", left_cos, own_cos, preferred_element_type=jnp.float32)
    pair_re = pair_re + jnp.einsum(
        "wki,wkj->ijk", left_sin, own_sin, preferred_element_type=jnp.float32
    )
    band_re = (pair_re * band_weight).astype(jnp.bfloat16)
    pair_im = jnp.einsum("wki,wkj->ijk", left_sin, own_cos, preferred_element_type=jnp.float32)
    pair_im = pair_im - jnp.einsum(
        "wki,wkj->ijk", left_cos, own_sin, preferred_element_type=jnp.float32
    )
    band_im = (pair_im * band_weight).astype(jnp.bfloat16)
    spectra = lax.all_to_all(
        jnp.stack((band_re, band_im)), "sta", split_axis=1, concat_axis=3, tiled=True
    )
    lag_count = LAGS
    transform = lag_table(freq_bins, lag_count)
    flat_spectra = spectra.reshape(2, recv_rows * stations, freq_bins)
    correlation = jnp.einsum(
        "cnk,ckt->nt", flat_spectra, transform, preferred_element_type=jnp.float32
    )
    block_row = lax.dynamic_index_in_dim(pair_mask, sta_index, 0, keepdims=False)
    station_row = jnp.repeat(block_row, recv_rows).astype(jnp.float32)
    receiver = sta_index * recv_rows + jnp.arange(recv_rows, dtype=jnp.int32)
    distinct = (receiver[:, None] != jnp.arange(stations, dtype=jnp.int32)[None, :]).astype(
        jnp.float32
    )
    pair_keep = station_row[None, :] * distinct
    correlation = correlation.reshape(recv_rows, stations, lag_count) * pair_keep[:, :, None]
    return lax.psum_scatter(correlation, "win", scatter_dimension=2, tiled=True)


def solution(mesh):
    def body(phases, window_valid, freq_taper, pair_mask):
        win_rows, band, stations = phases.shape
        sta_count, win_count = mesh.shape["sta"], mesh.shape["win"]
        power = band * sta_count & (band * sta_count - 1) == 0 and sta_count & (sta_count - 1) == 0
        if band % 128 == 0 and stations % 16 == 0 and win_count == 2 and power:
            return fused(phases, window_valid, freq_taper, pair_mask)
        return per_device(phases, window_valid, freq_taper, pair_mask)

    return jax.shard_map(
        body,
        mesh=mesh,
        in_specs=(P(("days", "win"), "sta", None), P("days"), P(), P()),
        out_specs=P(("days", "sta"), None, "win"),
        check_vma=False,
    )
```

```python
import math

import jax
import jax.numpy as jnp
import numpy as np
from jax import lax
from jax.experimental import pallas as pl
from jax.experimental.pallas import tpu as pltpu
from jax.sharding import PartitionSpec as P

LAGS = 512
MESH = pl.DeviceIdType.MESH


def fit(function, degree):
    nodes = np.polynomial.chebyshev.Chebyshev.interpolate(function, degree, domain=[0.0, math.pi**2])
    return [float(c) for c in nodes.convert(kind=np.polynomial.Polynomial).coef]


def sinc_of_square(y):
    x = np.sqrt(y)
    return np.sinc(x / math.pi)


SIN_COEF = fit(sinc_of_square, 7)
COS_COEF = fit(lambda y: np.cos(np.sqrt(y)), 8)


def horner(coef, y):
    total = jnp.full_like(y, coef[-1])
    for c in coef[-2::-1]:
        total = total * y + c
    return total


def cos_sin(x):
    y = x * x
    return horner(COS_COEF, y), x * horner(SIN_COEF, y)


def fused_kernel(
    phases_hbm,
    valid_hbm,
    taper_hbm,
    mask_hbm,
    out_ref,
    phases_ref,
    valid_ref,
    taper_ref,
    mask_ref,
    load_sem,
    cos_ref,
    sin_ref,
    spec_re,
    spec_im,
    lag_cos,
    lag_sin,
    own,
    swap_out,
    swap_in,
    send,
    recv,
    swap_send_sem,
    swap_recv_sem,
    send_sem,
    recv_sem,
    ready,
    *,
    sta_count,
):
    days, sta, win = (lax.axis_index(a) for a in ("days", "sta", "win"))
    win_rows, stations, band = phases_hbm.shape
    recv_rows = stations // sta_count
    block = recv_rows * stations
    freq_bins = band * sta_count
    half = LAGS // 2

    loads = [
        pltpu.make_async_copy(source, target, load_sem.at[n])
        for n, (source, target) in enumerate(
            (
                (phases_hbm, phases_ref),
                (valid_hbm, valid_ref),
                (taper_hbm, taper_ref),
                (mask_hbm, mask_ref),
            )
        )
    ]
    for load in loads:
        load.start()
    def across(step):
        bits = [2**n for n in range((sta_count - 1).bit_length())]
        return sum(lax.rem(lax.div(sta, n) + lax.div(jnp.int32(step), n), 2) * n for n in bits)

    barrier = pltpu.get_barrier_semaphore()
    for step in range(sta_count - 1, 0, -1):
        pl.semaphore_signal(barrier, inc=1, device_id=(days, across(step), 1), device_id_type=MESH)

    @pl.when(win == 1)
    def _():
        pl.semaphore_signal(barrier, inc=1, device_id=(days, sta, 0), device_id_type=MESH)

    rows = 16
    lag = lax.broadcasted_iota(jnp.int32, (rows, LAGS), 1) - half
    sub = lax.broadcasted_iota(jnp.int32, (rows, LAGS), 0)

    @pl.loop(0, band // rows)
    def _(b):
        k = sub + (sta * band + b * rows)
        turn = ((k * lag + freq_bins) & (2 * freq_bins - 1)) - freq_bins
        c, s = cos_sin(turn.astype(jnp.float32) * (math.pi / freq_bins))
        at = pl.ds(pl.multiple_of(b * rows, rows), rows)
        lag_cos[at, :] = c.astype(jnp.bfloat16)
        lag_sin[at, :] = (-s).astype(jnp.bfloat16)

    @pl.when(win == 0)
    def _():
        pl.semaphore_wait(barrier, 1)
        pl.semaphore_signal(ready, inc=1, device_id=(days, sta, 1), device_id_type=MESH)

    for load in loads:
        load.wait()

    for w in range(win_rows):
        weight = valid_ref[win * win_rows + w].astype(jnp.float32)
        c, s = cos_sin(phases_ref[w].astype(jnp.float32))
        cos_ref[w] = c.astype(jnp.bfloat16).astype(jnp.float32) * weight
        sin_ref[w] = s.astype(jnp.bfloat16).astype(jnp.float32) * weight

    count = valid_ref[0]
    for w in range(1, valid_ref.shape[0]):
        count = count + valid_ref[w]
    count = jnp.full((1, 128), count, jnp.int32).astype(jnp.float32)
    norm = 1.0 / jnp.sqrt(freq_bins * jnp.maximum(count, 1.0))
    lane_rows = band // 128
    weight = jnp.concatenate(
        [taper_ref[pl.ds(sta * lane_rows + r, 1), :] * norm for r in range(lane_rows)], axis=1
    )

    def swap(step):
        return pltpu.make_async_remote_copy(
            src_ref=swap_out.at[step],
            dst_ref=swap_in.at[step],
            send_sem=swap_send_sem.at[step],
            recv_sem=swap_recv_sem.at[step],
            device_id=(days, sta, 1 - win),
            device_id_type=MESH,
        )

    def scatter(step):
        peer = across(step)
        return pltpu.make_async_remote_copy(
            src_ref=send.at[peer],
            dst_ref=recv.at[step],
            send_sem=send_sem.at[step],
            recv_sem=recv_sem.at[step],
            device_id=(days, peer, win),
            device_id_type=MESH,
        )

    def cross(step):
        first = across(step) * recv_rows
        re = [jnp.zeros((stations, band), jnp.float32) for _ in range(recv_rows)]
        im = [jnp.zeros((stations, band), jnp.float32) for _ in range(recv_rows)]
        for w in range(win_rows):
            cj, sj = cos_ref[w], sin_ref[w]
            for q in range(recv_rows):
                ci = cos_ref[w, pl.ds(first + q, 1), :]
                si = sin_ref[w, pl.ds(first + q, 1), :]
                re[q] = re[q] + (ci * cj + si * sj)
                im[q] = im[q] + (si * cj - ci * sj)
        at = pl.ds(pl.multiple_of(first * stations, block), block)
        made = [
            jnp.concatenate([(x * weight).astype(jnp.bfloat16) for x in part], axis=0)
            for part in (re, im)
        ]
        spec_re[at, :], spec_im[at, :] = made
        return made

    def to_lags(re, im, which):
        at = pl.ds(pl.multiple_of(which * half, half), half)
        part = jnp.dot(re, lag_cos[:, at], preferred_element_type=jnp.float32)
        return part + jnp.dot(im, lag_sin[:, at], preferred_element_type=jnp.float32)

    def pack(step, re, im):
        swap_out[step] = to_lags(re, im, 1 - win).astype(jnp.bfloat16)

    @pl.when(win == 1)
    def _():
        pl.semaphore_wait(ready, 1)

    def chunk(n, before):
        step = sta_count - 1 - n
        pack(step + 1, *before)
        made = cross(step)
        swap(step + 1).start()
        return made

    pack(0, *lax.fori_loop(1, sta_count, chunk, cross(sta_count - 1)))
    mine = to_lags(spec_re[...], spec_im[...], win)
    swap(0).start()
    order = (7, 5, 3, 6, 4, 1, 2, 0)
    for b in range(sta_count):
        own[b] = mine[b * block : (b + 1) * block]

    @pl.when(win == 1)
    def _():
        pl.semaphore_wait(barrier, 2 * (sta_count - 1))
        pl.semaphore_signal(ready, inc=1, device_id=(days, sta, 0), device_id_type=MESH)

    @pl.when(win == 0)
    def _():
        pl.semaphore_wait(ready, 1)

    for step in order:
        peer = across(step)
        swap(step).wait_recv()
        total = own[peer] + swap_in[step].astype(jnp.float32)
        if step:
            send[peer] = total.astype(jnp.bfloat16)
            scatter(step).start()
    for step in range(1, sta_count):
        scatter(step).wait_recv()
        total = total + recv[step].astype(jnp.float32)

    source = lax.broadcasted_iota(jnp.int32, (stations, half), 0)
    keep = jnp.zeros((stations, half), jnp.float32)
    for b in range(sta_count):
        keep = jnp.where(source // recv_rows == b, mask_ref[sta, b].astype(jnp.float32), keep)
    for r in range(recv_rows):
        pair_keep = jnp.where(source == sta * recv_rows + r, 0.0, keep)
        out_ref[r] = total[r * stations : (r + 1) * stations] * pair_keep
    for step in order:
        swap(step).wait_send()
        if step:
            scatter(step).wait_send()


def fused(phases, window_valid, freq_taper, pair_mask):
    sta_count = lax.axis_size("sta")
    win_rows, band, stations = phases.shape
    recv_rows = stations // sta_count
    block = recv_rows * stations
    pairs = stations * stations
    half = LAGS // 2
    f32, bf16, vmem = jnp.float32, jnp.bfloat16, pltpu.VMEM
    return pl.pallas_call(
        lambda *refs: fused_kernel(*refs, sta_count=sta_count),
        name="fused",
        out_shape=jax.ShapeDtypeStruct((recv_rows, stations, half), f32),
        in_specs=[pl.BlockSpec(memory_space=pltpu.HBM)] * 4,
        out_specs=pl.BlockSpec(memory_space=pltpu.VMEM),
        scratch_shapes=[
            vmem((win_rows, stations, band), bf16),
            pltpu.SMEM(window_valid.shape, jnp.int32),
            vmem((freq_taper.shape[0] // 128, 128), f32),
            pltpu.SMEM(pair_mask.shape, jnp.int32),
            pltpu.SemaphoreType.DMA((4,)),
            vmem((win_rows, stations, band), f32),
            vmem((win_rows, stations, band), f32),
            vmem((pairs, band), bf16),
            vmem((pairs, band), bf16),
            vmem((band, LAGS), bf16),
            vmem((band, LAGS), bf16),
            vmem((sta_count, block, half), f32),
            vmem((sta_count, block, half), bf16),
            vmem((sta_count, block, half), bf16),
            vmem((sta_count, block, half), bf16),
            vmem((sta_count, block, half), bf16),
            pltpu.SemaphoreType.DMA((sta_count,)),
            pltpu.SemaphoreType.DMA((sta_count,)),
            pltpu.SemaphoreType.DMA((sta_count,)),
            pltpu.SemaphoreType.DMA((sta_count,)),
            pltpu.SemaphoreType.REGULAR,
        ],
        compiler_params=pltpu.CompilerParams(
            collective_id=0, has_side_effects=True, vmem_limit_bytes=16 * 2**20
        ),
    )(
        *(
            pltpu.with_memory_space_constraint(a, pltpu.HBM)
            for a in (
                jnp.transpose(phases, (0, 2, 1)),
                window_valid,
                freq_taper.reshape(-1, 128),
                pair_mask,
            )
        )
    )


def lag_table(freq_bins, lag_count):
    freq_index = jnp.arange(freq_bins, dtype=jnp.int32)[:, None]
    lag_index = jnp.arange(lag_count, dtype=jnp.int32)[None, :] - lag_count // 2
    wrapped = jnp.mod(freq_index * lag_index, 2 * freq_bins)
    angle = wrapped.astype(jnp.float32) * (math.pi / freq_bins)
    return jnp.stack((jnp.cos(angle), -jnp.sin(angle))).astype(jnp.bfloat16)


def per_device(phases, window_valid, freq_taper, pair_mask):
    sta_count = lax.axis_size("sta")
    win_rows, band_bins, stations = phases.shape
    freq_bins = band_bins * sta_count
    recv_rows = stations // sta_count
    sta_index = lax.axis_index("sta")
    win_group = lax.axis_index("win")
    valid_count = jnp.sum(window_valid.astype(jnp.float32))
    norm_scale = 1.0 / jnp.sqrt(freq_bins * jnp.maximum(valid_count, 1.0))
    bin_weight = freq_taper * norm_scale
    group_valid = lax.dynamic_slice_in_dim(window_valid, win_group * win_rows, win_rows)
    group_weight = group_valid.astype(jnp.bfloat16)[:, None, None]
    own_f = phases.astype(jnp.float32)
    own_cos = jnp.cos(own_f).astype(jnp.bfloat16)
    own_sin = jnp.sin(own_f).astype(jnp.bfloat16)
    left_cos = own_cos * group_weight
    left_sin = own_sin * group_weight
    band_weight = lax.dynamic_slice_in_dim(bin_weight, sta_index * band_bins, band_bins)
    pair_re = jnp.einsum("wki,wkj->ijk", left_cos, own_cos, preferred_element_type=jnp.float32)
    pair_re = pair_re + jnp.einsum(
        "wki,wkj->ijk", left_sin, own_sin, preferred_element_type=jnp.float32
    )
    band_re = (pair_re * band_weight).astype(jnp.bfloat16)
    pair_im = jnp.einsum("wki,wkj->ijk", left_sin, own_cos, preferred_element_type=jnp.float32)
    pair_im = pair_im - jnp.einsum(
        "wki,wkj->ijk", left_cos, own_sin, preferred_element_type=jnp.float32
    )
    band_im = (pair_im * band_weight).astype(jnp.bfloat16)
    spectra = lax.all_to_all(
        jnp.stack((band_re, band_im)), "sta", split_axis=1, concat_axis=3, tiled=True
    )
    lag_count = LAGS
    transform = lag_table(freq_bins, lag_count)
    flat_spectra = spectra.reshape(2, recv_rows * stations, freq_bins)
    correlation = jnp.einsum(
        "cnk,ckt->nt", flat_spectra, transform, preferred_element_type=jnp.float32
    )
    block_row = lax.dynamic_index_in_dim(pair_mask, sta_index, 0, keepdims=False)
    station_row = jnp.repeat(block_row, recv_rows).astype(jnp.float32)
    receiver = sta_index * recv_rows + jnp.arange(recv_rows, dtype=jnp.int32)
    distinct = (receiver[:, None] != jnp.arange(stations, dtype=jnp.int32)[None, :]).astype(
        jnp.float32
    )
    pair_keep = station_row[None, :] * distinct
    correlation = correlation.reshape(recv_rows, stations, lag_count) * pair_keep[:, :, None]
    return lax.psum_scatter(correlation, "win", scatter_dimension=2, tiled=True)


def solution(mesh):
    def body(phases, window_valid, freq_taper, pair_mask):
        win_rows, band, stations = phases.shape
        sta_count, win_count = mesh.shape["sta"], mesh.shape["win"]
        power = band * sta_count & (band * sta_count - 1) == 0 and sta_count & (sta_count - 1) == 0
        if sta_count == 8 and band % 128 == 0 and stations % 16 == 0 and win_count == 2 and power:
            return fused(phases, window_valid, freq_taper, pair_mask)
        return per_device(phases, window_valid, freq_taper, pair_mask)

    return jax.shard_map(
        body,
        mesh=mesh,
        in_specs=(P(("days", "win"), "sta", None), P("days"), P(), P()),
        out_specs=P(("days", "sta"), None, "win"),
        check_vma=False,
    )
```
